512 devices in a mesh: req: 128 (over z, y, core), tp: 4 (over x).
Axes of the slice: x: 4, y: 8, z: 8, core: 2. Of those that a mesh axis runs over, the one named last changes fastest.
Arguments:
- queries: bfloat16 [49152, 2048], P('req', 'tp'), may hold values from -32 to 32
- tree_kv: bfloat16 [49152, 256], P('req'), may hold values from -6 to 6
- suffix_kv: bfloat16 [768, 256, 256], P('req'), may hold values from -6 to 6
- suffix_len: int32 [768], P('req'), may hold values from 1 to 256
- group_ids: int32 [768], P('req'), may hold values from 0 to 1
- parents: int32 [768, 64], P('req'), may hold values from 0 to 62, as said below
- accepted: int32 [768, 8], P('req'), may hold values from 0 to 63, as said below
- prompt_kv: bfloat16 [2, 4096, 256], P(None, 'req'), may hold values from -12 to 12
- out_weight: bfloat16 [2048, 2048], P('tp'), may hold values from -0.5 to 0.5
Outputs:
- layer_output: bfloat16 [49152, 2048], P(('req', 'tp'))
- path_cache: bfloat16 [768, 8, 256], P('req')
The draws below stay inside these ranges and needn't reach their ends.
Inputs may be any that keep to these rules, and one draw needn't show every extreme that they name: parents[r, 0] = 0 and parents[r, i] < i for i >= 1, so node 0 is every tree's root. accepted[r] runs from the root down one branch: accepted[r, 0] = 0 and accepted[r, t - 1] = parents[r, accepted[r, t]].
All inputs are finite; a program needn't handle non-finite values.
Results may differ from the reference program's by a relative error of at most 0.017.
Values may be sent and summed in bfloat16 or wider, within the bound.
A program may use at most 64 MiB of HBM per device.

```python
import jax
import jax.numpy as jnp
from jax import lax

D = 2048
HEADS = 16
HD = 128
REQ_DEV = 6
TREE = 64
PATH = 8
SUF = 256
NGROUPS = 2
REQS = 768
TOKENS = 49152
PROMPT = 4096


def tree_helper(key):
    base = jax.random.fold_in(key, 5)
    first, second, third = jax.random.split(base, 3)
    steps = jax.random.randint(first, (REQS, TREE), 1, 5, dtype=jnp.int32)
    positions = jnp.arange(TREE, dtype=jnp.int32)
    parents = jnp.maximum(positions[None, :] - steps, 0)
    stride_top = max(1, (TREE - 1) // (PATH - 1))
    strides = jax.random.randint(second, (REQS, PATH - 1), 1, stride_top + 1, dtype=jnp.int32)
    nodes = jnp.concatenate([jnp.zeros((REQS, 1), jnp.int32), jnp.cumsum(strides, axis=1).astype(jnp.int32)], axis=1)
    forced = jax.random.randint(third, (), 0, REQS, dtype=jnp.int32)
    rows = jnp.arange(REQS, dtype=jnp.int32)
    last = jnp.where(rows == forced, TREE - 1, nodes[:, PATH - 1])
    accepted = jnp.concatenate([nodes[:, :PATH - 1], last[:, None]], axis=1)
    row_index = jnp.broadcast_to(rows[:, None], (REQS, PATH - 1))
    parents = parents.at[row_index, accepted[:, 1:]].set(accepted[:, :-1])
    return (parents, accepted)


def draw_parents(key, part):
    return tree_helper(key)[0]


def draw_accepted(key, part):
    return tree_helper(key)[1]


def draw_suffix_len(key, part):
    base = jax.random.fold_in(key, 11)
    first, second, third, fourth = jax.random.split(base, 4)
    device_count = REQS // REQ_DEV
    caps = jax.random.randint(first, (device_count,), max(1, SUF // 4), SUF + 1, dtype=jnp.int32)
    full_device = jax.random.randint(second, (), 0, device_count, dtype=jnp.int32)
    caps = jnp.where(jnp.arange(device_count, dtype=jnp.int32) == full_device, SUF, caps)
    raw = jax.random.randint(third, (device_count, REQ_DEV), 0, 1 << 20, dtype=jnp.int32) % caps[:, None] + 1
    full_slot = jax.random.randint(fourth, (device_count,), 0, REQ_DEV, dtype=jnp.int32)
    lengths = jnp.where(jnp.arange(REQ_DEV, dtype=jnp.int32)[None, :] == full_slot[:, None], caps[:, None], raw)
    return lengths.reshape(REQS)


def draw_queries(key, part):
    base = jax.random.fold_in(key, 21)
    return jnp.clip(2.0 * jax.random.normal(base, (TOKENS, D), jnp.float32), -12.0, 12.0).astype(jnp.bfloat16)


def draw_prompt_kv(key, part):
    base = jax.random.fold_in(key, 31)
    first = jax.random.fold_in(base, 0)
    shape = (NGROUPS, PROMPT, 2 * HD)
    return jnp.clip(jax.random.normal(first, shape, jnp.float32), -6.0, 6.0).astype(jnp.bfloat16)


def with_ends(array, rng, low, top_value):
    longest = array.shape.index(max(array.shape))
    spots = []
    for shift in (0, 1):
        where = [jax.random.randint(jax.random.fold_in(rng, axis), (), 0, length) for axis, length in enumerate(array.shape)]
        where[longest] = (where[longest] + shift) % array.shape[longest]
        spots.append(tuple(where))
    return array.at[spots[0]].set(low).at[spots[1]].set(top_value)


def levels(own_key, shape, shards, smallest, top_value):
    level = 1.0
    for dim, blocks in shards:
        heights = jax.random.uniform(jax.random.fold_in(jax.random.fold_in(own_key, 6), dim), (blocks,), jnp.float32, smallest / len(shards), top_value / len(shards))
        level = level * jnp.repeat(jnp.exp(heights), shape[dim] // blocks).reshape((-1,) + (1,) * (len(shape) - 1 - dim))
    return level


def gaussian(key, dims, deviation, limit, shards=(), held_as=jnp.bfloat16):
    entries = deviation * jax.random.normal(key, dims, jnp.float32)
    if shards:
        entries = entries * levels(key, dims, shards, -0.22, 0.18)
    return jnp.clip(entries, -limit, limit).astype(held_as)


def setup_inputs(seed: int = 0) -> dict:
    splits = jax.random.split(jax.random.key(seed), 10)
    return {
        "queries": draw_queries(jax.random.fold_in(splits[9], 71), 0),
        "tree_kv": gaussian(splits[1], (TOKENS, 2 * HD), 1.0, 6.0, ((0, 128),)),
        "suffix_kv": gaussian(splits[2], (REQS, SUF, 2 * HD), 1.0, 6.0, ((0, 128),)),
        "suffix_len": draw_suffix_len(jax.random.fold_in(splits[9], 71), 0),
        "group_ids": with_ends(jax.random.randint(splits[4], (REQS,), 0, NGROUPS), jax.random.fold_in(splits[4], 1), 0, NGROUPS - 1).astype(jnp.int32),
        "parents": draw_parents(jax.random.fold_in(splits[9], 71), 0),
        "accepted": draw_accepted(jax.random.fold_in(splits[9], 71), 0),
        "prompt_kv": draw_prompt_kv(jax.random.fold_in(splits[9], 71), 0),
        "out_weight": gaussian(splits[8], (D, D), HD ** -0.5, 0.5, ((0, 4),)),
    }


def ancestry(parents):
    node_count = parents.shape[1]
    positions = jnp.arange(node_count, dtype=jnp.int32)
    step_up = (parents[:, :, None] == positions[None, None, :]) & (positions[None, :, None] > 0)
    closure = jnp.where(step_up, 1.0, 0.0).astype(jnp.float32) + jnp.eye(node_count, dtype=jnp.float32)[None]
    for repeat in range(max(1, (node_count - 1).bit_length())):
        closure = jnp.minimum(closure + jnp.einsum('rij,rjk->rik', closure, closure, precision=lax.Precision.HIGHEST), 1.0)
    return closure > 0.5


def reference(queries, tree_kv, suffix_kv, suffix_len, group_ids, parents, accepted, prompt_kv, out_weight):
    closure = ancestry(parents)
    grouped = queries.reshape(REQS, TREE, HEADS, HD)
    own_keys = tree_kv.reshape(REQS, TREE, 2 * HD)
    slot_pos = jnp.arange(SUF, dtype=jnp.int32)

    def one_request(items):
        query_block, tree_block, suffix_block, length, group, related = items
        prompt_block = lax.dynamic_index_in_dim(prompt_kv, group, 0, keepdims=False)
        keys_all = jnp.concatenate([tree_block, suffix_block, prompt_block], axis=0).astype(jnp.float32)
        valid = jnp.concatenate([related, jnp.broadcast_to(slot_pos[None, :] < length, (TREE, SUF)),
                                 jnp.ones((TREE, PROMPT), dtype=bool)], axis=1)
        scores = jnp.einsum('thd,nd->thn', query_block.astype(jnp.float32), keys_all[:, :HD]) * (HD ** -0.5)
        scores = jnp.where(valid[:, None, :], scores, -jnp.inf)
        row_max = jnp.max(scores, axis=-1, keepdims=True)
        weights = jnp.where(valid[:, None, :], jnp.exp(scores - row_max), 0.0)
        rounded = lax.optimization_barrier(weights.astype(jnp.bfloat16)).astype(jnp.float32)
        summed = jnp.einsum('thn,nd->thd', rounded, keys_all[:, HD:])
        return (summed / jnp.sum(weights, axis=-1)[..., None]).astype(jnp.bfloat16)

    attended = lax.map(one_request, (grouped, own_keys, suffix_kv, suffix_len, group_ids, closure))
    layer_output = jnp.dot(attended.reshape(TOKENS, D), out_weight, preferred_element_type=jnp.float32).astype(jnp.bfloat16)
    path_cache = jnp.take_along_axis(own_keys, accepted[:, :, None], axis=1)
    return layer_output, path_cache
```

```python
import functools
import math

import jax
import jax.numpy as jnp
from jax import lax
from jax.experimental import pallas as pl
from jax.experimental.pallas import tpu as pltpu
from jax.sharding import PartitionSpec as P

MESH = pl.DeviceIdType.MESH
ring = 8
hd = 128
neg_large = -1e30
bf16 = jnp.bfloat16
f32 = jnp.float32


def dot(a, b):
    return jnp.dot(a, b, preferred_element_type=f32)


def dot_nt(a, b):
    return lax.dot_general(a, b, (((1,), (1,)), ((), ())), preferred_element_type=f32)


def dot_tn(a, b):
    return lax.dot_general(a, b, (((0,), (0,)), ((), ())), preferred_element_type=f32)


def kernel(
    len_ref, group_ref, parents_ref, accepted_ref, q_hbm, tree_hbm, suf_hbm, prompt_hbm, w_hbm,
    out_ref, path_ref,
    q_ref, tree_ref, suf_ref, w_ref, vt_ref, m_ref, acc_ref, part, half_in, full_in,
    local_sem, p1_send, p1_recv, p2_send, p2_recv, x_send, x_recv, rs_send, rs_recv, *prompt_refs,
):
    requests, nodes = parents_ref.shape
    heads = q_ref.shape[1] // hd
    cols = nodes * heads
    shard = prompt_hbm.shape[1]
    blk = ring * shard
    half = blk // 2
    mine, theirs = prompt_refs[:ring], prompt_refs[ring:]
    scale = math.log2(math.e) / math.sqrt(hd)

    me = lax.axis_index("req")
    tp = lax.axis_index("tp")
    core = lax.rem(me, 2)
    y = lax.rem(me // 2, ring)
    z = me // (2 * ring)

    def along(g, step):
        if g == 0:
            return (z * ring + lax.rem(y + step, ring)) * 2 + core
        return (lax.rem(z + step, ring) * ring + y) * 2 + core

    other = me + 1 - 2 * core
    right = lax.rem(tp + 1, 4)
    left = lax.rem(tp + 3, 4)

    locals_ = [
        pltpu.make_async_copy(prompt_hbm.at[0], mine[0].at[0, pl.ds(0, shard)], local_sem.at[0]),
        pltpu.make_async_copy(prompt_hbm.at[1], mine[0].at[1, pl.ds(0, shard)], local_sem.at[1]),
        pltpu.make_async_copy(q_hbm, q_ref, local_sem.at[2]),
        pltpu.make_async_copy(tree_hbm, tree_ref, local_sem.at[3]),
        pltpu.make_async_copy(suf_hbm, suf_ref, local_sem.at[4]),
        pltpu.make_async_copy(w_hbm, w_ref, local_sem.at[5]),
    ]
    for copy in locals_:
        copy.start()

    barrier = pltpu.get_barrier_semaphore()
    for g in (0, 1):
        for step in range(1, ring):
            pl.semaphore_signal(barrier, inc=1, device_id=(along(g, step), tp), device_id_type=MESH)
    pl.semaphore_signal(barrier, inc=1, device_id=(other, tp), device_id_type=MESH)
    pl.semaphore_signal(barrier, inc=1, device_id=(me, right), device_id_type=MESH)
    pl.semaphore_signal(barrier, inc=1, device_id=(me, left), device_id_type=MESH)
    pl.semaphore_wait(barrier, 2 * (ring - 1) + 3)

    def phase1(g, step):
        return pltpu.make_async_remote_copy(
            src_ref=prompt_hbm.at[g],
            dst_ref=mine[0].at[g, pl.ds(step * shard, shard)],
            send_sem=p1_send.at[g, step],
            recv_sem=p1_recv.at[g, step],
            device_id=(along(g, step), tp),
            device_id_type=MESH,
        )

    def phase2(g, slot, h):
        if slot < 4 or (slot == 4 and h == 0):
            source, target = slot - 1, along(1 - g, 1)
        else:
            source, target = (slot + 1) % ring, along(1 - g, ring - 1)
        return pltpu.make_async_remote_copy(
            src_ref=mine[source].at[g, pl.ds(h * half, half)],
            dst_ref=mine[slot].at[g, pl.ds(h * half, half)],
            send_sem=p2_send.at[g, slot, h],
            recv_sem=p2_recv.at[g, slot, h],
            device_id=(target, tp),
            device_id_type=MESH,
        )

    def exchange(g, slot, h):
        return pltpu.make_async_remote_copy(
            src_ref=mine[slot].at[g, pl.ds(h * half, half)],
            dst_ref=theirs[slot].at[g, pl.ds(h * half, half)],
            send_sem=x_send.at[g, slot, h],
            recv_sem=x_recv.at[g, slot, h],
            device_id=(other, tp),
            device_id_type=MESH,
        )

    started = []

    def start(copy):
        copy.start()
        started.append(copy)

    for step in (1, 7, 2, 6, 3, 5, 4):
        for g in (0, 1):
            start(phase1(g, step))

    eye = jnp.where(
        lax.broadcasted_iota(jnp.int32, (hd, hd), 0) == lax.broadcasted_iota(jnp.int32, (hd, hd), 1),
        1.0, 0.0,
    ).astype(bf16)

    def values_t(values):
        turned = dot_nt(eye, values).astype(bf16)
        return jnp.concatenate([turned, jnp.ones((16, values.shape[0]), bf16)], axis=0)

    def query(r):
        rows = pl.ds(pl.multiple_of(r * nodes, nodes), nodes)
        return jnp.concatenate(
            [q_ref[rows, h * hd : (h + 1) * hd] for h in range(heads)], axis=0
        )

    locals_[2].wait()
    locals_[3].wait()
    locals_[4].wait()

    row = lax.broadcasted_iota(jnp.int32, (nodes, nodes), 0)
    col = lax.broadcasted_iota(jnp.int32, (nodes, nodes), 1)
    spread = jnp.where(
        lax.broadcasted_iota(jnp.int32, (nodes, cols), 0)
        == lax.rem(lax.broadcasted_iota(jnp.int32, (nodes, cols), 1), nodes),
        1.0, 0.0,
    ).astype(bf16)
    node_path = lax.broadcasted_iota(jnp.int32, (nodes, accepted_ref.shape[1]), 0)
    closures = []
    for r in range(requests):
        up = (parents_ref[r : r + 1, :] == row) & (col > 0)
        closures.append(jnp.where(up | (row == col), 1.0, 0.0).astype(bf16))
    for repeat in range((nodes - 1).bit_length()):
        closures = [jnp.minimum(dot(c, c), 1.0).astype(bf16) for c in closures]
    slots = lax.broadcasted_iota(jnp.int32, (suf_ref.shape[1], cols), 0)
    for r in range(requests):
        related = dot(closures[r], spread) > 0.5
        tree = tree_ref[r * nodes : (r + 1) * nodes, :]
        q = query(r)
        s0 = jnp.where(related, dot_nt(tree[:, :hd], q), neg_large)
        s1 = jnp.where(slots < len_ref[r], dot_nt(suf_ref[r, :, :hd], q), neg_large)
        top = jnp.maximum(
            jnp.max(s0, axis=0, keepdims=True), jnp.max(s1, axis=0, keepdims=True)
        )
        p0 = jnp.exp2((s0 - top) * scale).astype(bf16)
        p1 = jnp.exp2((s1 - top) * scale).astype(bf16)
        m_ref[r] = top
        acc_ref[r] = dot(values_t(tree[:, hd:]), p0) + dot(values_t(suf_ref[r, :, hd:]), p1)
        chosen = jnp.where(node_path == accepted_ref[r : r + 1, :], 1.0, 0.0).astype(bf16)
        path_ref[r] = dot_tn(chosen, tree).astype(bf16)

    def absorb(pieces):
        for block in pieces:
            for g in (0, 1):
                vt_ref[block, g] = values_t(prompt_refs[block][g, :, hd:])

        def one(r):
            g = group_ref[r]
            q = query(r)
            scores = [dot_nt(prompt_refs[block][g, :, :hd], q) for block in pieces]
            before = m_ref[r]
            top = before
            for s in scores:
                top = jnp.maximum(top, jnp.max(s, axis=0, keepdims=True))
            total = acc_ref[r] * jnp.exp2((before - top) * scale)
            for s, block in zip(scores, pieces):
                weights = jnp.exp2((s - top) * scale).astype(bf16)
                total = total + dot(vt_ref[block, g], weights)
            m_ref[r] = top
            acc_ref[r] = total

        def body(pair, carry):
            one(2 * pair)
            one(2 * pair + 1)
            return carry

        lax.fori_loop(0, requests // 2, body, 0)

    locals_[0].wait()
    locals_[1].wait()
    for step in range(1, ring):
        for g in (0, 1):
            phase1(g, step).wait_recv()

    for h in (0, 1):
        for slot in (1, 7):
            for g in (0, 1):
                start(phase2(g, slot, h))
        for g in (0, 1):
            start(exchange(g, 0, h))
    for h in (0, 1):
        for g in (0, 1):
            exchange(g, 0, h).wait_recv()
    absorb([0, ring])

    for k in (1, 2, 3):
        for h in (0, 1):
            for slot in (k, ring - k):
                for g in (0, 1):
                    phase2(g, slot, h).wait_recv()
                    after = slot + 1 if slot < 4 else slot - 1
                    if after != 4 or (slot == 3) == (h == 0):
                        start(phase2(g, after, h))
                    start(exchange(g, slot, h))
        for h in (0, 1):
            for slot in (k, ring - k):
                for g in (0, 1):
                    exchange(g, slot, h).wait_recv()
        absorb([k, ring + k, ring - k, 2 * ring - k])
    for h in (0, 1):
        for g in (0, 1):
            phase2(g, 4, h).wait_recv()
            start(exchange(g, 4, h))
    for h in (0, 1):
        for g in (0, 1):
            exchange(g, 4, h).wait_recv()
    absorb([4, ring + 4])

    locals_[5].wait()

    def finish(r, carry):
        total = acc_ref[r]
        turned = (total[:hd] / total[hd : hd + 1]).T.astype(bf16)
        attended = jnp.concatenate(
            [turned[h * nodes : (h + 1) * nodes] for h in range(heads)], axis=1
        )
        rows = pl.ds(pl.multiple_of(r * nodes, nodes), nodes)
        part[rows, :] = dot(attended, w_ref[...]).astype(bf16)
        return carry

    lax.fori_loop(0, requests, finish, 0)

    rows_out = out_ref.shape[0]
    rows_half = rows_out // 2

    def block(device, h=None):
        if h is None:
            return pl.ds(pl.multiple_of(device * rows_out, 16), rows_out)
        return pl.ds(pl.multiple_of(device * rows_out + h * rows_half, 16), rows_half)

    across = lax.rem(tp + 2, 4)
    sides = (right, left)

    def scatter(stage, way):
        if stage == 0:
            source, target = part.at[block(across, way)], half_in.at[way]
        else:
            h = way if stage == 2 else 1 - way
            source = part.at[block(sides[way], h)]
            target = full_in.at[way, pl.ds(h * rows_half, rows_half)]
        return pltpu.make_async_remote_copy(
            src_ref=source,
            dst_ref=target,
            send_sem=rs_send.at[stage, way],
            recv_sem=rs_recv.at[stage, way],
            device_id=(me, sides[way]),
            device_id_type=MESH,
        )

    for stage in (0, 1):
        for way in (0, 1):
            start(scatter(stage, way))
    for way in (0, 1):
        scatter(0, way).wait_recv()
        rows = block(sides[way], way)
        part[rows, :] = (part[rows, :].astype(f32) + half_in[way].astype(f32)).astype(bf16)
        start(scatter(2, way))
    for stage in (1, 2):
        for way in (0, 1):
            scatter(stage, way).wait_recv()
    out_ref[...] = (
        part[block(tp), :].astype(f32) + full_in[0].astype(f32) + full_in[1].astype(f32)
    ).astype(bf16)
    for copy in started:
        copy.wait_send()


def local(
    queries, tree_kv, suffix_kv, suffix_len, group_ids, parents, accepted, prompt_kv, out_weight
):
    requests, nodes = parents.shape
    groups, shard, width = prompt_kv.shape
    heads = queries.shape[1] // hd
    cols = nodes * heads
    rows_out = queries.shape[0] // 4
    model = out_weight.shape[1]
    anywhere = pl.BlockSpec(memory_space=pl.ANY)
    smem = pl.BlockSpec(memory_space=pltpu.SMEM)
    vmem = pl.BlockSpec(memory_space=pltpu.VMEM)
    dma = pltpu.SemaphoreType.DMA
    return pl.pallas_call(
        kernel,
        out_shape=(
            jax.ShapeDtypeStruct((rows_out, model), bf16),
            jax.ShapeDtypeStruct((requests, accepted.shape[1], width), bf16),
        ),
        in_specs=[smem, smem, vmem, vmem] + [anywhere] * 5,
        out_specs=(vmem, vmem),
        scratch_shapes=[
            pltpu.VMEM(queries.shape, bf16),
            pltpu.VMEM(tree_kv.shape, bf16),
            pltpu.VMEM(suffix_kv.shape, bf16),
            pltpu.VMEM(out_weight.shape, bf16),
            pltpu.VMEM((2 * ring, groups, hd + 16, ring * shard), bf16),
            pltpu.VMEM((requests, 1, cols), f32),
            pltpu.VMEM((requests, hd + 16, cols), f32),
            pltpu.VMEM((queries.shape[0], model), bf16),
            pltpu.VMEM((2, rows_out // 2, model), bf16),
            pltpu.VMEM((2, rows_out, model), bf16),
            dma((6,)),
            dma((2, ring)),
            dma((2, ring)),
            dma((2, ring, 2)),
            dma((2, ring, 2)),
            dma((2, ring, 2)),
            dma((2, ring, 2)),
            dma((3, 2)),
            dma((3, 2)),
        ]
        + [pltpu.VMEM((groups, ring * shard, width), bf16)] * (2 * ring),
        compiler_params=pltpu.CompilerParams(
            collective_id=0, has_side_effects=True, vmem_limit_bytes=48 << 20
        ),
        name="verify_attention",
    )(
        suffix_len, group_ids, parents, accepted, queries, tree_kv, suffix_kv, prompt_kv, out_weight
    )


def solution(mesh):
    return jax.shard_map(
        local,
        mesh=mesh,
        in_specs=(
            P("req", "tp"),
            P("req", None),
            P("req", None, None),
            P("req"),
            P("req"),
            P("req", None),
            P("req", None),
            P(None, "req", None),
            P("tp", None),
        ),
        out_specs=(P(("req", "tp"), None), P("req", None, None)),
        check_vma=False,
    )
```

```python
import functools
import math

import jax
import jax.numpy as jnp
from jax import lax
from jax.experimental import pallas as pl
from jax.experimental.pallas import tpu as pltpu
from jax.sharding import PartitionSpec as P

MESH = pl.DeviceIdType.MESH
ring = 8
hd = 128
neg_large = -1e30
bf16 = jnp.bfloat16
f32 = jnp.float32


def dot(a, b):
    return jnp.dot(a, b, preferred_element_type=f32)


def dot_nt(a, b):
    return lax.dot_general(a, b, (((1,), (1,)), ((), ())), preferred_element_type=f32)


def dot_tn(a, b):
    return lax.dot_general(a, b, (((0,), (0,)), ((), ())), preferred_element_type=f32)


def kernel(
    len_hbm, group_hbm, parents_hbm, accepted_hbm, q_hbm, tree_hbm, suf_hbm, prompt_hbm, w_hbm,
    out_ref, path_ref,
    len_ref, group_ref, parents_ref, accepted_ref, q_ref, tree_ref, suf_ref, w_ref, vt_ref, m_ref, acc_ref, part, half_in, full_in,
    local_sem, p1_send, p1_recv, p2_send, p2_recv, x_send, x_recv, rs_send, rs_recv, *prompt_refs,
):
    requests, nodes = parents_ref.shape
    heads = q_ref.shape[1] // hd
    cols = nodes * heads
    shard = prompt_hbm.shape[1]
    blk = ring * shard
    half = blk // 2
    mine, theirs = prompt_refs[:ring], prompt_refs[ring:]
    scale = math.log2(math.e) / math.sqrt(hd)

    me = lax.axis_index("req")
    tp = lax.axis_index("tp")
    core = lax.rem(me, 2)
    y = lax.rem(me // 2, ring)
    z = me // (2 * ring)

    def along(g, step):
        if g == 0:
            return (z * ring + lax.rem(y + step, ring)) * 2 + core
        return (lax.rem(z + step, ring) * ring + y) * 2 + core

    other = me + 1 - 2 * core
    right = lax.rem(tp + 1, 4)
    left = lax.rem(tp + 3, 4)

    locals_ = [
        pltpu.make_async_copy(prompt_hbm.at[0], mine[0].at[0, pl.ds(0, shard)], local_sem.at[0]),
        pltpu.make_async_copy(prompt_hbm.at[1], mine[0].at[1, pl.ds(0, shard)], local_sem.at[1]),
        pltpu.make_async_copy(q_hbm, q_ref, local_sem.at[2]),
        pltpu.make_async_copy(tree_hbm, tree_ref, local_sem.at[3]),
        pltpu.make_async_copy(suf_hbm, suf_ref, local_sem.at[4]),
        pltpu.make_async_copy(w_hbm, w_ref, local_sem.at[5]),
        pltpu.make_async_copy(len_hbm, len_ref, local_sem.at[6]),
        pltpu.make_async_copy(group_hbm, group_ref, local_sem.at[7]),
        pltpu.make_async_copy(parents_hbm, parents_ref, local_sem.at[8]),
        pltpu.make_async_copy(accepted_hbm, accepted_ref, local_sem.at[9]),
    ]
    for copy in locals_:
        copy.start()

    barrier = pltpu.get_barrier_semaphore()
    for g in (0, 1):
        for step in range(1, ring):
            pl.semaphore_signal(barrier, inc=1, device_id=(along(g, step), tp), device_id_type=MESH)
    pl.semaphore_signal(barrier, inc=1, device_id=(other, tp), device_id_type=MESH)
    pl.semaphore_signal(barrier, inc=1, device_id=(me, right), device_id_type=MESH)
    pl.semaphore_signal(barrier, inc=1, device_id=(me, left), device_id_type=MESH)
    pl.semaphore_wait(barrier, 2 * (ring - 1) + 3)

    def phase1(g, step):
        return pltpu.make_async_remote_copy(
            src_ref=prompt_hbm.at[g],
            dst_ref=mine[0].at[g, pl.ds(step * shard, shard)],
            send_sem=p1_send.at[g, step],
            recv_sem=p1_recv.at[g, step],
            device_id=(along(g, step), tp),
            device_id_type=MESH,
        )

    def phase2(g, slot, h):
        if slot < 4 or (slot == 4 and h == 0):
            source, target = slot - 1, along(1 - g, 1)
        else:
            source, target = (slot + 1) % ring, along(1 - g, ring - 1)
        return pltpu.make_async_remote_copy(
            src_ref=mine[source].at[g, pl.ds(h * half, half)],
            dst_ref=mine[slot].at[g, pl.ds(h * half, half)],
            send_sem=p2_send.at[g, slot, h],
            recv_sem=p2_recv.at[g, slot, h],
            device_id=(target, tp),
            device_id_type=MESH,
        )

    def exchange(g, slot, h):
        return pltpu.make_async_remote_copy(
            src_ref=mine[slot].at[g, pl.ds(h * half, half)],
            dst_ref=theirs[slot].at[g, pl.ds(h * half, half)],
            send_sem=x_send.at[g, slot, h],
            recv_sem=x_recv.at[g, slot, h],
            device_id=(other, tp),
            device_id_type=MESH,
        )

    started = []

    def start(copy):
        copy.start()
        started.append(copy)

    for step in (1, 7, 2, 6, 3, 5, 4):
        for g in (0, 1):
            start(phase1(g, step))

    eye = jnp.where(
        lax.broadcasted_iota(jnp.int32, (hd, hd), 0) == lax.broadcasted_iota(jnp.int32, (hd, hd), 1),
        1.0, 0.0,
    ).astype(bf16)

    def values_t(values):
        turned = dot_nt(eye, values).astype(bf16)
        return jnp.concatenate([turned, jnp.ones((16, values.shape[0]), bf16)], axis=0)

    def query(r):
        rows = pl.ds(pl.multiple_of(r * nodes, nodes), nodes)
        return jnp.concatenate(
            [q_ref[rows, h * hd : (h + 1) * hd] for h in range(heads)], axis=0
        )

    for number in (2, 3, 4, 6, 7, 8, 9):
        locals_[number].wait()

    row = lax.broadcasted_iota(jnp.int32, (nodes, nodes), 0)
    col = lax.broadcasted_iota(jnp.int32, (nodes, nodes), 1)
    spread = jnp.where(
        lax.broadcasted_iota(jnp.int32, (nodes, cols), 0)
        == lax.rem(lax.broadcasted_iota(jnp.int32, (nodes, cols), 1), nodes),
        1.0, 0.0,
    ).astype(bf16)
    node_path = lax.broadcasted_iota(jnp.int32, (nodes, accepted_ref.shape[1]), 0)
    closures = []
    for r in range(requests):
        up = (parents_ref[r : r + 1, :] == row) & (col > 0)
        closures.append(jnp.where(up | (row == col), 1.0, 0.0).astype(bf16))
    for repeat in range((nodes - 1).bit_length()):
        closures = [jnp.minimum(dot(c, c), 1.0).astype(bf16) for c in closures]
    slots = lax.broadcasted_iota(jnp.int32, (suf_ref.shape[1], cols), 0)
    for r in range(requests):
        related = dot(closures[r], spread) > 0.5
        tree = tree_ref[r * nodes : (r + 1) * nodes, :]
        q = query(r)
        s0 = jnp.where(related, dot_nt(tree[:, :hd], q), neg_large)
        s1 = jnp.where(slots < len_ref[r], dot_nt(suf_ref[r, :, :hd], q), neg_large)
        top = jnp.maximum(
            jnp.max(s0, axis=0, keepdims=True), jnp.max(s1, axis=0, keepdims=True)
        )
        p0 = jnp.exp2((s0 - top) * scale).astype(bf16)
        p1 = jnp.exp2((s1 - top) * scale).astype(bf16)
        m_ref[r] = top
        acc_ref[r] = dot(values_t(tree[:, hd:]), p0) + dot(values_t(suf_ref[r, :, hd:]), p1)
        chosen = jnp.where(node_path == accepted_ref[r : r + 1, :], 1.0, 0.0).astype(bf16)
        path_ref[r] = dot_tn(chosen, tree).astype(bf16)

    def scores_of(pieces, r):
        g = group_ref[r]
        q = query(r)
        return [dot_nt(prompt_refs[block][g, :, :hd], q) for block in pieces]

    def update(pieces, r, scores):
        g = group_ref[r]
        before = m_ref[r]
        top = before
        for s in scores:
            top = jnp.maximum(top, jnp.max(s, axis=0, keepdims=True))
        total = acc_ref[r] * jnp.exp2((before - top) * scale)
        for s, block in zip(scores, pieces):
            weights = jnp.exp2((s - top) * scale).astype(bf16)
            total = total + dot(vt_ref[block, g], weights)
        return top, total

    def absorb(pieces, order=tuple(range(requests)), done=None):
        for block in pieces:
            for g in (0, 1):
                vt_ref[block, g] = values_t(prompt_refs[block][g, :, hd:])
        ahead = scores_of(pieces, order[0])
        for number, r in enumerate(order):
            scores = ahead
            if number + 1 < requests:
                ahead = scores_of(pieces, order[number + 1])
            top, total = update(pieces, r, scores)
            if done is None:
                m_ref[r] = top
                acc_ref[r] = total
            else:
                done(number, r, total)

    locals_[0].wait()
    locals_[1].wait()
    for step in range(1, ring):
        for g in (0, 1):
            phase1(g, step).wait_recv()

    for h in (0, 1):
        for slot in (1, 7):
            for g in (0, 1):
                start(phase2(g, slot, h))
        for g in (0, 1):
            start(exchange(g, 0, h))
    absorb([0])

    def pass_on(k):
        for h in (0, 1):
            for slot in (k, ring - k):
                for g in (0, 1):
                    phase2(g, slot, h).wait_recv()
                    after = slot + 1 if slot < 4 else slot - 1
                    if after != 4 or (slot == 3) == (h == 0):
                        start(phase2(g, after, h))
                    start(exchange(g, slot, h))

    def swapped(*slots):
        for slot in slots:
            for h in (0, 1):
                for g in (0, 1):
                    exchange(g, slot, h).wait_recv()

    pass_on(1)
    swapped(0)
    absorb([ring, 1, 7])
    pass_on(2)
    swapped(1, 7)
    absorb([ring + 1, ring + 7, 2, 6])
    pass_on(3)
    swapped(2, 6)
    absorb([ring + 2, ring + 6, 3, 5])
    for h in (0, 1):
        for g in (0, 1):
            phase2(g, 4, h).wait_recv()
            start(exchange(g, 4, h))
    swapped(3, 5)
    absorb([ring + 3, ring + 5, 4])
    swapped(4)
    locals_[5].wait()

    rows_out = out_ref.shape[0]
    rows_half = rows_out // 2

    def block(device, h=None):
        if h is None:
            return pl.ds(pl.multiple_of(device * rows_out, 16), rows_out)
        return pl.ds(pl.multiple_of(device * rows_out + h * rows_half, 16), rows_half)

    across = lax.rem(tp + 2, 4)

    def scatter(stage, way):
        side = lax.rem(tp + 1 + 2 * way, 4)
        if stage == 0:
            source, target = part.at[block(across, way)], half_in.at[way]
        else:
            h = way if stage == 2 else 1 - way
            source = part.at[block(side, h)]
            target = full_in.at[way, pl.ds(pl.multiple_of(h * rows_half, 16), rows_half)]
        return pltpu.make_async_remote_copy(
            src_ref=source,
            dst_ref=target,
            send_sem=rs_send.at[stage, way],
            recv_sem=rs_recv.at[stage, way],
            device_id=(me, side),
            device_id_type=MESH,
        )

    odd = lax.rem(tp, 2)
    near = 1 - odd
    first = 3 * lax.rem(tp // 2 + 1, 2)
    second = 3 - first
    order = (
        first + 2 * odd, first + 1, first + 2 - 2 * odd,
        second + 1, second + 2 - 2 * odd, second + 2 * odd,
    )

    def finish(number, r, total):
        turned = (total[:hd] * (1.0 / total[hd : hd + 1])).T.astype(bf16)
        attended = jnp.concatenate(
            [turned[h * nodes : (h + 1) * nodes] for h in range(heads)], axis=1
        )
        rows = pl.ds(pl.multiple_of(r * nodes, nodes), nodes)
        part[rows, :] = dot(attended, w_ref[...]).astype(bf16)
        if number == 1:
            for way in (0, 1):
                start(scatter(0, way))
        if number == 2:
            start(scatter(1, near))
        if number == 4:
            start(scatter(1, 1 - near))

    absorb([ring + 4], order, finish)

    for way in (0, 1):
        scatter(0, way).wait_recv()
        rows = block(lax.rem(tp + 1 + 2 * way, 4), way)
        part[rows, :] = (part[rows, :].astype(f32) + half_in[way].astype(f32)).astype(bf16)
        start(scatter(2, way))
    for stage in (1, 2):
        for way in (0, 1):
            scatter(stage, way).wait_recv()
    out_ref[...] = (
        part[block(tp), :].astype(f32) + full_in[0].astype(f32) + full_in[1].astype(f32)
    ).astype(bf16)
    for copy in started:
        copy.wait_send()


def local(
    queries, tree_kv, suffix_kv, suffix_len, group_ids, parents, accepted, prompt_kv, out_weight
):
    requests, nodes = parents.shape
    groups, shard, width = prompt_kv.shape
    heads = queries.shape[1] // hd
    cols = nodes * heads
    rows_out = queries.shape[0] // 4
    model = out_weight.shape[1]
    hbm = pl.BlockSpec(memory_space=pltpu.HBM)
    vmem = pl.BlockSpec(memory_space=pltpu.VMEM)
    dma = pltpu.SemaphoreType.DMA
    return pl.pallas_call(
        kernel,
        out_shape=(
            jax.ShapeDtypeStruct((rows_out, model), bf16),
            jax.ShapeDtypeStruct((requests, accepted.shape[1], width), bf16),
        ),
        in_specs=[hbm] * 9,
        out_specs=(vmem, vmem),
        scratch_shapes=[
            pltpu.SMEM(suffix_len.shape, jnp.int32),
            pltpu.SMEM(group_ids.shape, jnp.int32),
            pltpu.VMEM(parents.shape, jnp.int32),
            pltpu.VMEM(accepted.shape, jnp.int32),
            pltpu.VMEM(queries.shape, bf16),
            pltpu.VMEM(tree_kv.shape, bf16),
            pltpu.VMEM(suffix_kv.shape, bf16),
            pltpu.VMEM(out_weight.shape, bf16),
            pltpu.VMEM((2 * ring, groups, hd + 16, ring * shard), bf16),
            pltpu.VMEM((requests, 1, cols), f32),
            pltpu.VMEM((requests, hd + 16, cols), f32),
            pltpu.VMEM((queries.shape[0], model), bf16),
            pltpu.VMEM((2, rows_out // 2, model), bf16),
            pltpu.VMEM((2, rows_out, model), bf16),
            dma((10,)),
            dma((2, ring)),
            dma((2, ring)),
            dma((2, ring, 2)),
            dma((2, ring, 2)),
            dma((2, ring, 2)),
            dma((2, ring, 2)),
            dma((3, 2)),
            dma((3, 2)),
        ]
        + [pltpu.VMEM((groups, ring * shard, width), bf16)] * (2 * ring),
        compiler_params=pltpu.CompilerParams(
            collective_id=0, has_side_effects=True, vmem_limit_bytes=62 << 20
        ),
        name="verify_attention",
    )(
        suffix_len, group_ids, parents, accepted, queries, tree_kv, suffix_kv, prompt_kv, out_weight
    )


def solution(mesh):
    return jax.shard_map(
        local,
        mesh=mesh,
        in_specs=(
            P("req", "tp"),
            P("req", None),
            P("req", None, None),
            P("req"),
            P("req"),
            P("req", None),
            P("req", None),
            P(None, "req", None),
            P("tp", None),
        ),
        out_specs=(P(("req", "tp"), None), P("req", None, None)),
        check_vma=False,
    )
```

```python
import functools
import math

import jax
import jax.numpy as jnp
from jax import lax
from jax.experimental import pallas as pl
from jax.experimental.pallas import tpu as pltpu
from jax.sharding import PartitionSpec as P

MESH = pl.DeviceIdType.MESH
ring = 8
places = {0: 0, 1: 1, 7: 2, 2: 3, 6: 4, 3: 5, 5: 6, 4: 7}
hd = 128
neg_large = -1e30
bf16 = jnp.bfloat16
f32 = jnp.float32


def dot(a, b):
    return jnp.dot(a, b, preferred_element_type=f32)


def dot_nt(a, b):
    return lax.dot_general(a, b, (((1,), (1,)), ((), ())), preferred_element_type=f32)


def dot_tn(a, b):
    return lax.dot_general(a, b, (((0,), (0,)), ((), ())), preferred_element_type=f32)


def kernel(
    len_hbm, group_hbm, parents_hbm, accepted_hbm, q_hbm, tree_hbm, suf_hbm, prompt_hbm, w_hbm,
    out_ref, path_ref,
    len_ref, group_ref, parents_ref, accepted_ref, q_ref, tree_ref, suf_ref, w_ref, vt_ref, m_ref, acc_ref, part, half_in, full_in,
    local_sem, p1_send, p1_recv, p2_send, p2_recv, x_send, x_recv, rs_send, rs_recv, *prompt_refs,
):
    requests, nodes = parents_ref.shape
    heads = q_ref.shape[1] // hd
    cols = nodes * heads
    shard = prompt_hbm.shape[1]
    blk = ring * shard
    half = blk // 2
    mine, theirs = prompt_refs[:ring], prompt_refs[ring:]
    scale = math.log2(math.e) / math.sqrt(hd)

    me = lax.axis_index("req")
    tp = lax.axis_index("tp")
    core = lax.rem(me, 2)
    y = lax.rem(me // 2, ring)
    z = me // (2 * ring)

    def along(g, step):
        if g == 0:
            return (z * ring + lax.rem(y + step, ring)) * 2 + core
        return (lax.rem(z + step, ring) * ring + y) * 2 + core

    other = me + 1 - 2 * core
    right = lax.rem(tp + 1, 4)
    left = lax.rem(tp + 3, 4)

    locals_ = [
        pltpu.make_async_copy(prompt_hbm.at[0], mine[0].at[0, pl.ds(0, shard)], local_sem.at[0]),
        pltpu.make_async_copy(prompt_hbm.at[1], mine[0].at[1, pl.ds(0, shard)], local_sem.at[1]),
        pltpu.make_async_copy(q_hbm, q_ref, local_sem.at[2]),
        pltpu.make_async_copy(tree_hbm, tree_ref, local_sem.at[3]),
        pltpu.make_async_copy(suf_hbm, suf_ref, local_sem.at[4]),
        pltpu.make_async_copy(w_hbm, w_ref, local_sem.at[5]),
        pltpu.make_async_copy(len_hbm, len_ref, local_sem.at[6]),
        pltpu.make_async_copy(group_hbm, group_ref, local_sem.at[7]),
        pltpu.make_async_copy(parents_hbm, parents_ref, local_sem.at[8]),
        pltpu.make_async_copy(accepted_hbm, accepted_ref, local_sem.at[9]),
    ]
    for copy in locals_:
        copy.start()

    barrier = pltpu.get_barrier_semaphore()
    for g in (0, 1):
        for step in range(1, ring):
            pl.semaphore_signal(barrier, inc=1, device_id=(along(g, step), tp), device_id_type=MESH)
    pl.semaphore_signal(barrier, inc=1, device_id=(other, tp), device_id_type=MESH)
    pl.semaphore_signal(barrier, inc=1, device_id=(me, right), device_id_type=MESH)
    pl.semaphore_signal(barrier, inc=1, device_id=(me, left), device_id_type=MESH)
    pl.semaphore_wait(barrier, 2 * (ring - 1) + 3)

    def phase1(g, step):
        return pltpu.make_async_remote_copy(
            src_ref=prompt_hbm.at[g],
            dst_ref=mine[0].at[g, pl.ds(places[step] * shard, shard)],
            send_sem=p1_send.at[g, step],
            recv_sem=p1_recv.at[g, step],
            device_id=(along(g, step), tp),
            device_id_type=MESH,
        )

    def phase2(g, slot, h):
        if slot < 4 or (slot == 4 and h == 0):
            source, target = slot - 1, along(1 - g, 1)
        else:
            source, target = (slot + 1) % ring, along(1 - g, ring - 1)
        return pltpu.make_async_remote_copy(
            src_ref=mine[source].at[g, pl.ds(h * half, half)],
            dst_ref=mine[slot].at[g, pl.ds(h * half, half)],
            send_sem=p2_send.at[g, slot, h],
            recv_sem=p2_recv.at[g, slot, h],
            device_id=(target, tp),
            device_id_type=MESH,
        )

    def exchange(g, slot, h):
        return pltpu.make_async_remote_copy(
            src_ref=mine[slot].at[g, pl.ds(h * half, half)],
            dst_ref=theirs[slot].at[g, pl.ds(h * half, half)],
            send_sem=x_send.at[g, slot, h],
            recv_sem=x_recv.at[g, slot, h],
            device_id=(other, tp),
            device_id_type=MESH,
        )

    started = []

    def start(copy):
        copy.start()
        started.append(copy)

    for step in (4, 3, 5, 6, 2, 1, 7):
        for g in (0, 1):
            start(phase1(g, step))

    eye = jnp.where(
        lax.broadcasted_iota(jnp.int32, (hd, hd), 0) == lax.broadcasted_iota(jnp.int32, (hd, hd), 1),
        1.0, 0.0,
    ).astype(bf16)

    def values_t(values):
        turned = dot_nt(eye, values).astype(bf16)
        return jnp.concatenate([turned, jnp.ones((16, values.shape[0]), bf16)], axis=0)

    def query(r):
        rows = pl.ds(pl.multiple_of(r * nodes, nodes), nodes)
        return jnp.concatenate(
            [q_ref[rows, h * hd : (h + 1) * hd] for h in range(heads)], axis=0
        )

    for number in (2, 3, 4, 6, 7, 8, 9):
        locals_[number].wait()

    row = lax.broadcasted_iota(jnp.int32, (nodes, nodes), 0)
    col = lax.broadcasted_iota(jnp.int32, (nodes, nodes), 1)
    spread = jnp.where(
        lax.broadcasted_iota(jnp.int32, (nodes, cols), 0)
        == lax.rem(lax.broadcasted_iota(jnp.int32, (nodes, cols), 1), nodes),
        1.0, 0.0,
    ).astype(bf16)
    node_path = lax.broadcasted_iota(jnp.int32, (nodes, accepted_ref.shape[1]), 0)
    closures = []
    for r in range(requests):
        up = (parents_ref[r : r + 1, :] == row) & (col > 0)
        closures.append(jnp.where(up | (row == col), 1.0, 0.0).astype(bf16))
    for repeat in range((nodes - 1).bit_length()):
        closures = [jnp.minimum(dot(c, c), 1.0).astype(bf16) for c in closures]
    slots = lax.broadcasted_iota(jnp.int32, (suf_ref.shape[1], cols), 0)

    def set_off(h, steps):
        for step in steps:
            for g in (0, 1):
                phase1(g, step).wait_recv()
        for slot in (1, 7):
            for g in (0, 1):
                start(phase2(g, slot, h))
        for g in (0, 1):
            start(exchange(g, 0, h))

    for r in range(requests):
        if r == requests // 2:
            locals_[0].wait()
            locals_[1].wait()
            set_off(0, (1, 7, 2))
        related = dot(closures[r], spread) > 0.5
        tree = tree_ref[r * nodes : (r + 1) * nodes, :]
        q = query(r)
        s0 = jnp.where(related, dot_nt(tree[:, :hd], q), neg_large)
        s1 = jnp.where(slots < len_ref[r], dot_nt(suf_ref[r, :, :hd], q), neg_large)
        top = jnp.maximum(
            jnp.max(s0, axis=0, keepdims=True), jnp.max(s1, axis=0, keepdims=True)
        )
        p0 = jnp.exp2((s0 - top) * scale).astype(bf16)
        p1 = jnp.exp2((s1 - top) * scale).astype(bf16)
        m_ref[r] = top
        acc_ref[r] = dot(values_t(tree[:, hd:]), p0) + dot(values_t(suf_ref[r, :, hd:]), p1)
        chosen = jnp.where(node_path == accepted_ref[r : r + 1, :], 1.0, 0.0).astype(bf16)
        path_ref[r] = dot_tn(chosen, tree).astype(bf16)

    def scores_of(pieces, r):
        g = group_ref[r]
        q = query(r)
        return [dot_nt(prompt_refs[block][g, :, :hd], q) for block in pieces]

    def update(pieces, r, scores):
        g = group_ref[r]
        before = m_ref[r]
        top = before
        for s in scores:
            top = jnp.maximum(top, jnp.max(s, axis=0, keepdims=True))
        total = acc_ref[r] * jnp.exp2((before - top) * scale)
        for s, block in zip(scores, pieces):
            weights = jnp.exp2((s - top) * scale).astype(bf16)
            total = total + dot(vt_ref[block, g], weights)
        return top, total

    def absorb(pieces, order=tuple(range(requests)), done=None):
        for block in pieces:
            for g in (0, 1):
                vt_ref[block, g] = values_t(prompt_refs[block][g, :, hd:])
        ahead = scores_of(pieces, order[0])
        for number, r in enumerate(order):
            scores = ahead
            if number + 1 < requests:
                ahead = scores_of(pieces, order[number + 1])
            top, total = update(pieces, r, scores)
            if done is None:
                m_ref[r] = top
                acc_ref[r] = total
            else:
                done(number, r, total)

    def pass_on(k, h):
        for slot in (k, ring - k):
            for g in (0, 1):
                phase2(g, slot, h).wait_recv()
                after = slot + 1 if slot < 4 else slot - 1
                if after != 4 or (slot == 3) == (h == 0):
                    start(phase2(g, after, h))
        for slot in (k, ring - k):
            for g in (0, 1):
                start(exchange(g, slot, h))

    def last(h):
        for g in (0, 1):
            phase2(g, 4, h).wait_recv()
            start(exchange(g, 4, h))

    def swapped(*slots):
        for slot in slots:
            for h in (0, 1):
                for g in (0, 1):
                    exchange(g, slot, h).wait_recv()

    set_off(1, (6, 3, 5, 4))
    absorb([0])
    pass_on(1, 0)
    swapped(0)
    absorb([ring])
    pass_on(1, 1)
    absorb([1, 7])
    pass_on(2, 0)
    swapped(1, 7)
    absorb([ring + 1, ring + 7])
    pass_on(2, 1)
    absorb([2, 6])
    pass_on(3, 0)
    swapped(2, 6)
    absorb([ring + 2, ring + 6])
    pass_on(3, 1)
    absorb([3, 5])
    last(0)
    swapped(3, 5)
    absorb([ring + 3, ring + 5])
    last(1)
    absorb([4])
    swapped(4)
    locals_[5].wait()

    rows_out = out_ref.shape[0]
    rows_half = rows_out // 2

    def block(device, h=None):
        if h is None:
            return pl.ds(pl.multiple_of(device * rows_out, 16), rows_out)
        return pl.ds(pl.multiple_of(device * rows_out + h * rows_half, 16), rows_half)

    across = lax.rem(tp + 2, 4)

    def scatter(stage, way):
        side = lax.rem(tp + 1 + 2 * way, 4)
        if stage == 0:
            source, target = part.at[block(across, way)], half_in.at[way]
        else:
            h = way if stage == 2 else 1 - way
            source = part.at[block(side, h)]
            target = full_in.at[way, pl.ds(pl.multiple_of(h * rows_half, 16), rows_half)]
        return pltpu.make_async_remote_copy(
            src_ref=source,
            dst_ref=target,
            send_sem=rs_send.at[stage, way],
            recv_sem=rs_recv.at[stage, way],
            device_id=(me, side),
            device_id_type=MESH,
        )

    odd = lax.rem(tp, 2)
    first = 3 * lax.rem(tp // 2 + 1, 2)
    second = 3 - first
    order = (
        first + 2 * odd, first + 1, first + 2 - 2 * odd,
        second + 1, second + 2 - 2 * odd, second + 2 * odd,
    )

    held = []

    def finish(number, r, total):
        turned = (total[:hd] * (1.0 / total[hd : hd + 1])).T.astype(bf16)
        held.append((r, jnp.concatenate(
            [turned[h * nodes : (h + 1) * nodes] for h in range(heads)], axis=1
        )))
        if number in (0, 3):
            return
        projected = dot(jnp.concatenate([a for _, a in held], axis=0), w_ref[...]).astype(bf16)
        for at, (r, _) in enumerate(held):
            rows = pl.ds(pl.multiple_of(r * nodes, nodes), nodes)
            part[rows, :] = projected[at * nodes : (at + 1) * nodes]
        held.clear()
        if number == 1:
            for way in (0, 1):
                scatter(0, way).start()

    absorb([ring + 4], order, finish)

    for way in (0, 1):
        scatter(0, way).wait_send()
        start(scatter(1, way))
    for way in (0, 1):
        scatter(0, way).wait_recv()
        rows = block(lax.rem(tp + 1 + 2 * way, 4), way)
        part[rows, :] = (part[rows, :].astype(f32) + half_in[way].astype(f32)).astype(bf16)
        start(scatter(2, way))
    for stage in (1, 2):
        for way in (0, 1):
            scatter(stage, way).wait_recv()
    out_ref[...] = (
        part[block(tp), :].astype(f32) + full_in[0].astype(f32) + full_in[1].astype(f32)
    ).astype(bf16)
    for copy in started:
        copy.wait_send()


def local(
    queries, tree_kv, suffix_kv, suffix_len, group_ids, parents, accepted, prompt_kv, out_weight
):
    requests, nodes = parents.shape
    groups, shard, width = prompt_kv.shape
    heads = queries.shape[1] // hd
    cols = nodes * heads
    rows_out = queries.shape[0] // 4
    model = out_weight.shape[1]
    hbm = pl.BlockSpec(memory_space=pltpu.HBM)
    vmem = pl.BlockSpec(memory_space=pltpu.VMEM)
    dma = pltpu.SemaphoreType.DMA
    return pl.pallas_call(
        kernel,
        out_shape=(
            jax.ShapeDtypeStruct((rows_out, model), bf16),
            jax.ShapeDtypeStruct((requests, accepted.shape[1], width), bf16),
        ),
        in_specs=[hbm] * 9,
        out_specs=(vmem, vmem),
        scratch_shapes=[
            pltpu.SMEM(suffix_len.shape, jnp.int32),
            pltpu.SMEM(group_ids.shape, jnp.int32),
            pltpu.VMEM(parents.shape, jnp.int32),
            pltpu.VMEM(accepted.shape, jnp.int32),
            pltpu.VMEM(queries.shape, bf16),
            pltpu.VMEM(tree_kv.shape, bf16),
            pltpu.VMEM(suffix_kv.shape, bf16),
            pltpu.VMEM(out_weight.shape, bf16),
            pltpu.VMEM((2 * ring, groups, hd + 16, ring * shard), bf16),
            pltpu.VMEM((requests, 1, cols), f32),
            pltpu.VMEM((requests, hd + 16, cols), f32),
            pltpu.VMEM((queries.shape[0], model), bf16),
            pltpu.VMEM((2, rows_out // 2, model), bf16),
            pltpu.VMEM((2, rows_out, model), bf16),
            dma((10,)),
            dma((2, ring)),
            dma((2, ring)),
            dma((2, ring, 2)),
            dma((2, ring, 2)),
            dma((2, ring, 2)),
            dma((2, ring, 2)),
            dma((3, 2)),
            dma((3, 2)),
        ]
        + [pltpu.VMEM((groups, ring * shard, width), bf16)] * (2 * ring),
        compiler_params=pltpu.CompilerParams(
            collective_id=0, has_side_effects=True, vmem_limit_bytes=62 << 20
        ),
        name="verify_attention",
    )(
        suffix_len, group_ids, parents, accepted, queries, tree_kv, suffix_kv, prompt_kv, out_weight
    )


def solution(mesh):
    return jax.shard_map(
        local,
        mesh=mesh,
        in_specs=(
            P("req", "tp"),
            P("req", None),
            P("req", None, None),
            P("req"),
            P("req"),
            P("req", None),
            P("req", None),
            P(None, "req", None),
            P("tp", None),
        ),
        out_specs=(P(("req", "tp"), None), P("req", None, None)),
        check_vma=False,
    )
```

```python
import functools
import math

import jax
import jax.numpy as jnp
from jax import lax
from jax.experimental import pallas as pl
from jax.experimental.pallas import tpu as pltpu
from jax.sharding import PartitionSpec as P

MESH = pl.DeviceIdType.MESH
ring = 8
places = {0: 0, 1: 1, 7: 2, 2: 3, 6: 4, 3: 5, 5: 6, 4: 7}
hd = 128
neg_large = -1e30
bf16 = jnp.bfloat16
f32 = jnp.float32


def dot(a, b):
    return jnp.dot(a, b, preferred_element_type=f32)


def dot_nt(a, b):
    return lax.dot_general(a, b, (((1,), (1,)), ((), ())), preferred_element_type=f32)


def dot_tn(a, b):
    return lax.dot_general(a, b, (((0,), (0,)), ((), ())), preferred_element_type=f32)


def kernel(
    len_hbm, group_hbm, parents_hbm, accepted_hbm, q_hbm, tree_hbm, suf_hbm, prompt_hbm, w_hbm,
    out_ref, path_ref,
    len_ref, group_ref, parents_ref, accepted_ref, q_ref, tree_ref, suf_ref, w_ref, vt_ref, m_ref, acc_ref, part, half_in, full_in,
    local_sem, p1_send, p1_recv, p2_send, p2_recv, x_send, x_recv, rs_send, rs_recv, *prompt_refs,
):
    requests, nodes = parents_ref.shape
    heads = q_ref.shape[1] // hd
    cols = nodes * heads
    shard = prompt_hbm.shape[1]
    blk = ring * shard
    half = blk // 2
    mine, theirs = prompt_refs[:ring], prompt_refs[ring:]
    scale = math.log2(math.e) / math.sqrt(hd)

    me = lax.axis_index("req")
    tp = lax.axis_index("tp")
    core = lax.rem(me, 2)
    y = lax.rem(me // 2, ring)
    z = me // (2 * ring)

    def along(g, step):
        if g == 0:
            return (z * ring + lax.rem(y + step, ring)) * 2 + core
        return (lax.rem(z + step, ring) * ring + y) * 2 + core

    other = me + 1 - 2 * core
    right = lax.rem(tp + 1, 4)
    left = lax.rem(tp + 3, 4)

    locals_ = [
        pltpu.make_async_copy(prompt_hbm.at[0], mine[0].at[0, pl.ds(0, shard)], local_sem.at[0]),
        pltpu.make_async_copy(prompt_hbm.at[1], mine[0].at[1, pl.ds(0, shard)], local_sem.at[1]),
        pltpu.make_async_copy(q_hbm, q_ref, local_sem.at[2]),
        pltpu.make_async_copy(tree_hbm, tree_ref, local_sem.at[3]),
        pltpu.make_async_copy(suf_hbm, suf_ref, local_sem.at[4]),
        pltpu.make_async_copy(w_hbm, w_ref, local_sem.at[5]),
        pltpu.make_async_copy(len_hbm, len_ref, local_sem.at[6]),
        pltpu.make_async_copy(group_hbm, group_ref, local_sem.at[7]),
        pltpu.make_async_copy(parents_hbm, parents_ref, local_sem.at[8]),
        pltpu.make_async_copy(accepted_hbm, accepted_ref, local_sem.at[9]),
    ]
    for copy in locals_:
        copy.start()

    barrier = pltpu.get_barrier_semaphore()
    for g in (0, 1):
        for step in range(1, ring):
            pl.semaphore_signal(barrier, inc=1, device_id=(along(g, step), tp), device_id_type=MESH)
    pl.semaphore_signal(barrier, inc=1, device_id=(other, tp), device_id_type=MESH)
    pl.semaphore_signal(barrier, inc=1, device_id=(me, right), device_id_type=MESH)
    pl.semaphore_signal(barrier, inc=1, device_id=(me, left), device_id_type=MESH)
    pl.semaphore_wait(barrier, 2 * (ring - 1) + 3)

    def phase1(g, step):
        return pltpu.make_async_remote_copy(
            src_ref=prompt_hbm.at[g],
            dst_ref=mine[0].at[g, pl.ds(places[step] * shard, shard)],
            send_sem=p1_send.at[g, step],
            recv_sem=p1_recv.at[g, step],
            device_id=(along(g, step), tp),
            device_id_type=MESH,
        )

    def phase2(g, slot, h):
        if slot < 4 or (slot == 4 and h == 0):
            source, target = slot - 1, along(1 - g, 1)
        else:
            source, target = (slot + 1) % ring, along(1 - g, ring - 1)
        return pltpu.make_async_remote_copy(
            src_ref=mine[source].at[g, pl.ds(h * half, half)],
            dst_ref=mine[slot].at[g, pl.ds(h * half, half)],
            send_sem=p2_send.at[g, slot, h],
            recv_sem=p2_recv.at[g, slot, h],
            device_id=(target, tp),
            device_id_type=MESH,
        )

    def exchange(g, slot, h):
        return pltpu.make_async_remote_copy(
            src_ref=mine[slot].at[g, pl.ds(h * half, half)],
            dst_ref=theirs[slot].at[g, pl.ds(h * half, half)],
            send_sem=x_send.at[g, slot, h],
            recv_sem=x_recv.at[g, slot, h],
            device_id=(other, tp),
            device_id_type=MESH,
        )

    started = []

    def start(copy):
        copy.start()
        started.append(copy)

    for step in (4, 3, 5, 6, 2, 1, 7):
        for g in (0, 1):
            start(phase1(g, step))

    eye = jnp.where(
        lax.broadcasted_iota(jnp.int32, (hd, hd), 0) == lax.broadcasted_iota(jnp.int32, (hd, hd), 1),
        1.0, 0.0,
    ).astype(bf16)

    def values_t(values):
        turned = dot_nt(eye, values).astype(bf16)
        return jnp.concatenate([turned, jnp.ones((16, values.shape[0]), bf16)], axis=0)

    def query(r):
        rows = pl.ds(pl.multiple_of(r * nodes, nodes), nodes)
        return jnp.concatenate(
            [q_ref[rows, h * hd : (h + 1) * hd] for h in range(heads)], axis=0
        )

    for number in (2, 3, 4, 6, 7, 8, 9):
        locals_[number].wait()

    row = lax.broadcasted_iota(jnp.int32, (nodes, nodes), 0)
    col = lax.broadcasted_iota(jnp.int32, (nodes, nodes), 1)
    spread = jnp.where(
        lax.broadcasted_iota(jnp.int32, (nodes, cols), 0)
        == lax.rem(lax.broadcasted_iota(jnp.int32, (nodes, cols), 1), nodes),
        1.0, 0.0,
    ).astype(bf16)
    node_path = lax.broadcasted_iota(jnp.int32, (nodes, accepted_ref.shape[1]), 0)
    closures = []
    for r in range(requests):
        up = (parents_ref[r : r + 1, :] == row) & (col > 0)
        closures.append(jnp.where(up | (row == col), 1.0, 0.0).astype(bf16))
    for repeat in range((nodes - 1).bit_length()):
        closures = [jnp.minimum(dot(c, c), 1.0).astype(bf16) for c in closures]
    slots = lax.broadcasted_iota(jnp.int32, (suf_ref.shape[1], cols), 0)

    def set_off(h, steps):
        for step in steps:
            for g in (0, 1):
                phase1(g, step).wait_recv()
        for slot in (1, 7):
            for g in (0, 1):
                start(phase2(g, slot, h))
        for g in (0, 1):
            start(exchange(g, 0, h))

    for r in range(requests):
        if r == requests // 2:
            locals_[0].wait()
            locals_[1].wait()
            set_off(0, (1, 7, 2))
        related = dot(closures[r], spread) > 0.5
        tree = tree_ref[r * nodes : (r + 1) * nodes, :]
        q = query(r)
        s0 = jnp.where(related, dot_nt(tree[:, :hd], q), neg_large)
        s1 = jnp.where(slots < len_ref[r], dot_nt(suf_ref[r, :, :hd], q), neg_large)
        top = jnp.maximum(
            jnp.max(s0, axis=0, keepdims=True), jnp.max(s1, axis=0, keepdims=True)
        )
        p0 = jnp.exp2((s0 - top) * scale).astype(bf16)
        p1 = jnp.exp2((s1 - top) * scale).astype(bf16)
        m_ref[r] = top
        acc_ref[r] = dot(values_t(tree[:, hd:]), p0) + dot(values_t(suf_ref[r, :, hd:]), p1)
        chosen = jnp.where(node_path == accepted_ref[r : r + 1, :], 1.0, 0.0).astype(bf16)
        path_ref[r] = dot_tn(chosen, tree).astype(bf16)

    def scores_of(pieces, r):
        g = group_ref[r]
        q = query(r)
        return [dot_nt(prompt_refs[block][g, :, :hd], q) for block in pieces]

    def update(pieces, r, scores):
        g = group_ref[r]
        before = m_ref[r]
        top = before
        for s in scores:
            top = jnp.maximum(top, jnp.max(s, axis=0, keepdims=True))
        total = acc_ref[r] * jnp.exp2((before - top) * scale)
        for s, block in zip(scores, pieces):
            weights = jnp.exp2((s - top) * scale).astype(bf16)
            total = total + dot(vt_ref[block, g], weights)
        return top, total

    def turn(pieces):
        for block in pieces:
            for g in (0, 1):
                vt_ref[block, g] = values_t(prompt_refs[block][g, :, hd:])

    def absorb(pieces, order=tuple(range(requests)), done=None, fresh=True):
        if fresh:
            turn(pieces)
            pieces = [pieces] * len(order)
        ahead = scores_of(pieces[0], order[0])
        for number, r in enumerate(order):
            scores = ahead
            if number + 1 < len(order):
                ahead = scores_of(pieces[number + 1], order[number + 1])
            top, total = update(pieces[number], r, scores)
            if done is None:
                m_ref[r] = top
                acc_ref[r] = total
            else:
                done(number, r, total)

    def pass_on(k, h):
        for slot in (k, ring - k):
            for g in (0, 1):
                phase2(g, slot, h).wait_recv()
                after = slot + 1 if slot < 4 else slot - 1
                if after != 4 or (slot == 3) == (h == 0):
                    start(phase2(g, after, h))
        for slot in (k, ring - k):
            for g in (0, 1):
                start(exchange(g, slot, h))

    def last(h):
        for g in (0, 1):
            phase2(g, 4, h).wait_recv()
            start(exchange(g, 4, h))

    def swapped(*slots):
        for slot in slots:
            for h in (0, 1):
                for g in (0, 1):
                    exchange(g, slot, h).wait_recv()

    set_off(1, (6, 3, 5, 4))
    absorb([0])
    pass_on(1, 0)
    swapped(0)
    absorb([ring])
    pass_on(1, 1)
    absorb([1, 7])
    pass_on(2, 0)
    swapped(1, 7)
    absorb([ring + 1, ring + 7])
    pass_on(2, 1)
    absorb([2, 6])
    pass_on(3, 0)
    swapped(2, 6)
    absorb([ring + 2, ring + 6])
    pass_on(3, 1)
    absorb([3, 5])
    last(0)
    swapped(3, 5)
    absorb([ring + 3, ring + 5])
    last(1)
    locals_[5].wait()

    rows_out = out_ref.shape[0]
    rows_half = rows_out // 2

    def block(device, h=None):
        if h is None:
            return pl.ds(pl.multiple_of(device * rows_out, 16), rows_out)
        return pl.ds(pl.multiple_of(device * rows_out + h * rows_half, 16), rows_half)

    across = lax.rem(tp + 2, 4)

    def scatter(stage, way):
        side = lax.rem(tp + 1 + 2 * way, 4)
        if stage == 0:
            source, target = part.at[block(across, way)], half_in.at[way]
        else:
            h = way if stage == 2 else 1 - way
            source = part.at[block(side, h)]
            target = full_in.at[way, pl.ds(pl.multiple_of(h * rows_half, 16), rows_half)]
        return pltpu.make_async_remote_copy(
            src_ref=source,
            dst_ref=target,
            send_sem=rs_send.at[stage, way],
            recv_sem=rs_recv.at[stage, way],
            device_id=(me, side),
            device_id_type=MESH,
        )

    odd = lax.rem(tp, 2)
    first = 3 * lax.rem(tp // 2 + 1, 2)
    second = 3 - first
    order = (
        first + 2 * odd, first + 1, first + 2 - 2 * odd,
        second + 1, second + 2 - 2 * odd, second + 2 * odd,
    )

    held = []

    def finish(number, r, total):
        turned = (total[:hd] * (1.0 / total[hd : hd + 1])).T.astype(bf16)
        held.append((r, jnp.concatenate(
            [turned[h * nodes : (h + 1) * nodes] for h in range(heads)], axis=1
        )))
        if number in (0, 3):
            return
        projected = dot(jnp.concatenate([a for _, a in held], axis=0), w_ref[...]).astype(bf16)
        for at, (r, _) in enumerate(held):
            rows = pl.ds(pl.multiple_of(r * nodes, nodes), nodes)
            part[rows, :] = projected[at * nodes : (at + 1) * nodes]
        held.clear()
        if number == 1:
            for way in (0, 1):
                scatter(0, way).start()

    absorb([4], order[:2])
    swapped(4)
    turn([ring + 4])
    absorb([[ring + 4]] * 2 + [[4, ring + 4]] * (requests - 2), order, finish, False)

    for way in (0, 1):
        scatter(0, way).wait_send()
        start(scatter(1, way))
    for way in (0, 1):
        scatter(0, way).wait_recv()
        rows = block(lax.rem(tp + 1 + 2 * way, 4), way)
        part[rows, :] = (part[rows, :].astype(f32) + half_in[way].astype(f32)).astype(bf16)
        start(scatter(2, way))
    for stage in (1, 2):
        for way in (0, 1):
            scatter(stage, way).wait_recv()
    out_ref[...] = (
        part[block(tp), :].astype(f32) + full_in[0].astype(f32) + full_in[1].astype(f32)
    ).astype(bf16)
    for copy in started:
        copy.wait_send()


def local(
    queries, tree_kv, suffix_kv, suffix_len, group_ids, parents, accepted, prompt_kv, out_weight
):
    requests, nodes = parents.shape
    groups, shard, width = prompt_kv.shape
    heads = queries.shape[1] // hd
    cols = nodes * heads
    rows_out = queries.shape[0] // 4
    model = out_weight.shape[1]
    hbm = pl.BlockSpec(memory_space=pltpu.HBM)
    vmem = pl.BlockSpec(memory_space=pltpu.VMEM)
    dma = pltpu.SemaphoreType.DMA
    return pl.pallas_call(
        kernel,
        out_shape=(
            jax.ShapeDtypeStruct((rows_out, model), bf16),
            jax.ShapeDtypeStruct((requests, accepted.shape[1], width), bf16),
        ),
        in_specs=[hbm] * 9,
        out_specs=(vmem, vmem),
        scratch_shapes=[
            pltpu.SMEM(suffix_len.shape, jnp.int32),
            pltpu.SMEM(group_ids.shape, jnp.int32),
            pltpu.VMEM(parents.shape, jnp.int32),
            pltpu.VMEM(accepted.shape, jnp.int32),
            pltpu.VMEM(queries.shape, bf16),
            pltpu.VMEM(tree_kv.shape, bf16),
            pltpu.VMEM(suffix_kv.shape, bf16),
            pltpu.VMEM(out_weight.shape, bf16),
            pltpu.VMEM((2 * ring, groups, hd + 16, ring * shard), bf16),
            pltpu.VMEM((requests, 1, cols), f32),
            pltpu.VMEM((requests, hd + 16, cols), f32),
            pltpu.VMEM((queries.shape[0], model), bf16),
            pltpu.VMEM((2, rows_out // 2, model), bf16),
            pltpu.VMEM((2, rows_out, model), bf16),
            dma((10,)),
            dma((2, ring)),
            dma((2, ring)),
            dma((2, ring, 2)),
            dma((2, ring, 2)),
            dma((2, ring, 2)),
            dma((2, ring, 2)),
            dma((3, 2)),
            dma((3, 2)),
        ]
        + [pltpu.VMEM((groups, ring * shard, width), bf16)] * (2 * ring),
        compiler_params=pltpu.CompilerParams(
            collective_id=0, has_side_effects=True, vmem_limit_bytes=62 << 20
        ),
        name="verify_attention",
    )(
        suffix_len, group_ids, parents, accepted, queries, tree_kv, suffix_kv, prompt_kv, out_weight
    )


def solution(mesh):
    return jax.shard_map(
        local,
        mesh=mesh,
        in_specs=(
            P("req", "tp"),
            P("req", None),
            P("req", None, None),
            P("req"),
            P("req"),
            P("req", None),
            P("req", None),
            P(None, "req", None),
            P("tp", None),
        ),
        out_specs=(P(("req", "tp"), None), P("req", None, None)),
        check_vma=False,
    )
```
